128 devices in a mesh: fsdp: 32 (over y_hi, z, x), ctx: 4 (over y_lo, core).
Axes of the slice: x: 4, y: 4 (y_hi: 2, y_lo: 2; y = y_hi * 2 + y_lo), z: 4, core: 2. Of those that a mesh axis runs over, the one named last changes fastest.
Arguments:
- loaded: bfloat16 [32768, 12288], P(('fsdp', 'ctx')), may hold values from -6 to 6
- route: int32 [128, 32], P(('fsdp', 'ctx')), may hold values from 0 to 31, each once within a row
- doc_ids: int32 [32, 1024], P('fsdp'), may hold values from 0 to 7, never falling along the last dimension, each value on 1 to 512 neighbouring positions
- short_filter: float32 [7, 768], replicated, may hold values from -2 to 2
- medium_filter: bfloat16 [128, 256], replicated, may hold values from -0.5 to 0.5
- out_weight: bfloat16 [4096, 8192], P('fsdp', 'ctx'), may hold values from -0.09375 to 0.09375
Outputs:
- mixed: bfloat16 [32768, 8192], P(('fsdp', 'ctx'))
The draws below stay inside these ranges and needn't reach their ends.
Inputs may be any that keep to these rules, and one draw needn't show every extreme that they name: Each row of route names every sequence 0 to 31 exactly once. `doc_ids`: along each sequence the document numbers never fall; each document spans 1 to 512 positions and one spans exactly 512.
All inputs are finite; a program needn't handle non-finite values.
Results may differ from the reference program's by a relative error of at most 0.0058.
Values may be sent and summed in bfloat16 or wider, within the bound.
A program may use at most 128 MiB of HBM per device.

```python
import math
import jax
import jax.numpy as jnp
import numpy as np
from jax import lax

D = 8192
CH = 4096
GSIZE = 16
KS = 7
KM = 128
DOCS = 8
LEN = 1024
TOKENS = 32768
BLK = 8
SGROUPS = 768
MGROUPS = 256
DOC_MOST = 512
N_FSDP = 32
N_CTX = 4


def block_levels(rng, shape, pieces, low, largest):
    def one(position, shards_of):
        heights = jax.random.uniform(jax.random.fold_in(jax.random.fold_in(rng, 6), position), (shards_of,), jnp.float32, low / len(pieces), largest / len(pieces))
        return jnp.repeat(jnp.exp(heights), shape[position] // shards_of).reshape((-1,) + (1,) * (len(shape) - position - 1))

    gain = one(*pieces[0])
    for cut in pieces[1:]:
        gain = gain * one(*cut)
    return gain


def length_profile(amount, total, reach, lean):
    weights = [(1 << 20) // math.isqrt(rank ** lean) + 1 for rank in range(2, amount + 1)]
    rest, holding = total - reach - (amount - 1), [1] * (amount - 1)
    while rest > 0:
        free = [i for i in range(amount - 1) if holding[i] < reach]
        whole, budget = sum([weights[i] for i in free]), rest
        for i in free:
            extra = min(reach - holding[i], max(1, budget * weights[i] // whole), rest)
            holding[i] = holding[i] + extra
            rest = rest - extra
    return np.array([reach] + holding)


def uneven_parts(rng, number_of, total, most, slope):
    if number_of == 2:
        one = jax.random.randint(rng, (), max(1, total - most), min(most, total - 1) + 1)
        return jnp.stack([one, total - one])
    tallies = jnp.asarray(length_profile(number_of, total, most, slope), jnp.int32)
    twos = (number_of - 1) // 2
    source_of, taker = tallies[1:1 + 2 * twos:2], tallies[2:2 + 2 * twos:2]
    margin = jnp.minimum(source_of - 1, most - taker)
    moved = jax.random.randint(jax.random.fold_in(rng, 1), (twos,), 0, 1 << 20) % (margin + 1)
    tallies = tallies.at[1:1 + 2 * twos:2].set(source_of - moved).at[2:2 + 2 * twos:2].set(taker + moved)
    return tallies[jax.random.permutation(jax.random.fold_in(rng, 2), number_of)]


def gaussian(stream_key, dims, width, most, split=(), held_as=jnp.bfloat16):
    entries = jax.random.normal(stream_key, dims, jnp.float32) * width
    if len(split) > 0:
        entries = block_levels(stream_key, dims, split, -0.22, 0.18) * entries
    return jnp.clip(entries, min=-most, max=most).astype(held_as)


def setup_inputs(seed: int = 0) -> dict:
    key_of = jax.random.split(jax.random.key(seed), 7)
    return {
        "loaded": gaussian(key_of[0], (TOKENS, 3 * CH), 1.0, 6.0, ((0, 128),)),
        "route": jax.vmap(lambda own: jax.random.permutation(own, N_FSDP))(jax.random.split(key_of[1], (N_FSDP * N_CTX))).reshape((N_FSDP * N_CTX, N_FSDP)).astype(jnp.int32),
        "doc_ids": jax.vmap(lambda own: jnp.searchsorted(jnp.cumsum(uneven_parts(own, DOCS, LEN, DOC_MOST, 2)), jnp.arange(LEN), side="right"))(jax.random.split(key_of[2], N_FSDP)).reshape((N_FSDP, LEN)).astype(jnp.int32),
        "short_filter": gaussian(key_of[3], (KS, SGROUPS), KS ** -0.5, 2.0, (), jnp.float32),
        "medium_filter": gaussian(key_of[4], (KM, MGROUPS), KM ** -0.5, 0.5),
        "out_weight": gaussian(key_of[5], (CH, D), CH ** -0.5, 0.09375, ((0, 32), (1, 4))),
    }


def reference(loaded, route, doc_ids, short_filter, medium_filter, out_weight):
    blocks = loaded.reshape(N_FSDP, N_CTX, N_FSDP, BLK, 3 * CH)
    inverse = jnp.argsort(route.reshape(N_FSDP, N_CTX, N_FSDP), axis=-1).astype(jnp.int32)
    short_full = jnp.repeat(short_filter.astype(jnp.float32), GSIZE, axis=1)
    medium_full = jnp.repeat(medium_filter.astype(jnp.float32), GSIZE, axis=1)
    loader_rows = jnp.arange(N_FSDP, dtype=jnp.int32)[:, None]
    context_cols = jnp.arange(N_CTX, dtype=jnp.int32)[None, :]

    def one_sequence(owner_row):
        picked = inverse[:, :, owner_row]
        gathered = blocks[loader_rows, context_cols, picked]
        features = jnp.transpose(gathered, (1, 0, 2, 3)).reshape(LEN, 3 * CH).astype(jnp.float32)
        doc_rows = doc_ids[owner_row]
        short_pad = jnp.concatenate([jnp.zeros((KS - 1, 3 * CH), jnp.float32), features], axis=0)
        short_ids = jnp.concatenate([jnp.full((KS - 1,), -1, jnp.int32), doc_rows], axis=0)
        summed = jnp.zeros((LEN, 3 * CH), jnp.float32)
        for offset in range(KS):
            shifted = short_pad[KS - 1 - offset: KS - 1 - offset + LEN]
            same_doc = (short_ids[KS - 1 - offset: KS - 1 - offset + LEN] == doc_rows).astype(jnp.float32)[:, None]
            summed = summed + short_full[offset][None, :] * shifted * same_doc
        query = summed[:, :CH]
        gate_in = (summed[:, CH:2 * CH] * summed[:, 2 * CH:]).astype(jnp.bfloat16)
        gate_pad = jnp.concatenate([jnp.zeros((KM - 1, CH), jnp.float32), gate_in.astype(jnp.float32)], axis=0)
        gate_ids = jnp.concatenate([jnp.full((KM - 1,), -1, jnp.int32), doc_rows], axis=0)

        def add_offset(offset, running):
            first_row = (KM - 1 - offset).astype(jnp.int32)
            shifted = lax.dynamic_slice_in_dim(gate_pad, first_row, LEN, 0)
            shift_ids = lax.dynamic_slice_in_dim(gate_ids, first_row, LEN, 0)
            same_doc = (shift_ids == doc_rows).astype(jnp.float32)[:, None]
            filter_tap = lax.dynamic_slice_in_dim(medium_full, offset.astype(jnp.int32), 1, 0)
            return running + filter_tap * shifted * same_doc

        medium = lax.fori_loop(0, KM, add_offset, jnp.zeros((LEN, CH), jnp.float32))
        gated = (query * medium).astype(jnp.bfloat16)
        return jnp.dot(gated, out_weight, preferred_element_type=jnp.float32).astype(jnp.bfloat16)

    outputs = lax.map(one_sequence, jnp.arange(N_FSDP, dtype=jnp.int32))
    return outputs.reshape(TOKENS, D)
```

```python
import functools

import jax
import jax.numpy as jnp
from jax import lax
from jax.experimental import pallas as pl
from jax.experimental.pallas import tpu as pltpu
from jax.sharding import PartitionSpec as P

MESH = pl.DeviceIdType.MESH
VMEM_LIMIT = 66_000_000
RING = 4
WAVES = 4
TILE = 256
BLOCK = 128
GROUP = 16
TAPS = 7
CHUNK = 512
BUFFERS = 4


def pick_kernel(order, loaded, picked, held, load_sem, store_sem):
    blocks = loaded.shape[0]

    def load(i, start):
        copy = pltpu.make_async_copy(loaded.at[order[i]], held.at[i], load_sem.at[i])
        copy.start() if start else copy.wait()

    def store(i, start):
        copy = pltpu.make_async_copy(held.at[i], picked.at[i], store_sem.at[i])
        copy.start() if start else copy.wait()

    @pl.loop(0, blocks)
    def _(i):
        load(i, True)

    @pl.loop(0, blocks)
    def _(i):
        load(i, False)
        store(i, True)

    @pl.loop(0, blocks)
    def _(i):
        store(i, False)


def pick_blocks(order, loaded):
    blocks, rows, wide = loaded.shape
    return pl.pallas_call(
        pick_kernel,
        out_shape=jax.ShapeDtypeStruct(loaded.shape, loaded.dtype),
        in_specs=[
            pl.BlockSpec(memory_space=pltpu.SMEM),
            pl.BlockSpec(memory_space=pl.ANY),
        ],
        out_specs=pl.BlockSpec(memory_space=pl.ANY),
        scratch_shapes=[
            pltpu.VMEM((blocks, rows, wide), loaded.dtype),
            pltpu.SemaphoreType.DMA((blocks,)),
            pltpu.SemaphoreType.DMA((blocks,)),
        ],
        compiler_params=pltpu.CompilerParams(vmem_limit_bytes=VMEM_LIMIT),
        name="pick_blocks",
    )(order, loaded)


def band_kernel(base_ref, mask_ref, out_ref):
    def one(j, carry):
        row = jnp.broadcast_to(base_ref[pl.ds(j, 1), :], (BLOCK, 2 * BLOCK))
        band = pltpu.roll(row, 0, 1, stride=1, stride_axis=0)
        start = pl.multiple_of(j * BLOCK, BLOCK)
        for b in range(2):
            out_ref[0, b, pl.ds(start, BLOCK), :] = (band * mask_ref[b]).astype(jnp.bfloat16)
        return carry

    lax.fori_loop(0, GROUP, one, 0)


def build_bands(base, mask):
    groups = base.shape[0]
    tiles = groups // GROUP
    return pl.pallas_call(
        band_kernel,
        out_shape=jax.ShapeDtypeStruct((tiles, 2, GROUP * BLOCK, 2 * BLOCK), jnp.bfloat16),
        grid=(tiles,),
        in_specs=[
            pl.BlockSpec((GROUP, 2 * BLOCK), lambda t: (t, 0)),
            pl.BlockSpec((2, BLOCK, 2 * BLOCK), lambda t: (0, 0, 0)),
        ],
        out_specs=pl.BlockSpec((1, 2, GROUP * BLOCK, 2 * BLOCK), lambda t: (t, 0, 0, 0)),
        cost_estimate=pl.CostEstimate(
            flops=groups * BLOCK * BLOCK * 8, bytes_accessed=groups * BLOCK * BLOCK * 8, transcendentals=0
        ),
        name="build_bands",
    )(base, mask)


def mixer_kernel(
    owned, bands, short_mask, short_full, weight, out,
    w_all, gated, staged, rows, feat, gate, xk, band_buf,
    ys, yr, d1s, d1r, d2s, d2r, e1s, e1r, e2s, e2r,
    fs, fr, hs, hr, ns, nr, ss, sr, gs, gr, cs, cr, ls, bs, os,
):
    fsdp, ctx = lax.axis_index("fsdp"), lax.axis_index("ctx")
    yh, zc, xc = fsdp // (RING * RING), (fsdp // RING) % RING, fsdp % RING
    sib, nb = (fsdp, ctx ^ 1), (fsdp, ctx ^ 2)
    after, before = (fsdp, (ctx + 1) % 4), (fsdp, (ctx + 3) % 4)
    partner = ((1 - yh) * RING * RING + zc * RING + xc, ctx)
    channels = gated.shape[2]
    tiles = channels // TILE
    chunks = channels // CHUNK
    tok = owned.shape[0]

    def coords(h):
        return (xc, zc) if h == 0 else (zc, xc)

    def dev(h, a, b):
        a, b = (a + RING) % RING, (b + RING) % RING
        z, x = (b, a) if h == 0 else (a, b)
        return (yh * RING * RING + z * RING + x, ctx)

    def piece(w, h, y, a, b):
        a, b = (a + RING) % RING, (b + RING) % RING
        z, x = (b, a) if h == 0 else (a, b)
        return w_all.at[w, h, y, z, x]

    def panel(w, h, y, b):
        b = (b + RING) % RING
        if h == 0:
            return w_all.at[w, h, y, b]
        return w_all.at[w, h, y, :, b]

    def panels(w, h, b):
        b = (b + RING) % RING
        if h == 0:
            return w_all.at[w, h, :, b]
        return w_all.at[w, h, :, :, b]

    def shard(w, h):
        return weight.at[:, pl.ds(w * CHUNK + h * TILE, TILE)]

    def remote(src, dst, send, recv, to):
        return pltpu.make_async_remote_copy(
            src_ref=src, dst_ref=dst, send_sem=send, recv_sem=recv, device_id=to, device_id_type=MESH
        )

    halves = [(w, h) for w in range(WAVES) for h in range(2)]
    ways = ((0, 1), (1, -1))

    def y_copy(w, h):
        a, b = coords(h)
        return remote(shard(w, h), piece(w, h, yh, a, b), ys.at[w, h], yr.at[w, h], partner)

    def y_got(w, h):
        a, b = coords(h)
        return remote(shard(w, h), piece(w, h, 1 - yh, a, b), ys.at[w, h], yr.at[w, h], partner)

    def d1_copy(w, h, d, step, other):
        a, b = coords(h)
        y = 1 - yh if other else yh
        src = piece(w, h, y, a, b) if other else shard(w, h)
        return remote(src, piece(w, h, y, a, b), d1s.at[w, h, d, other], d1r.at[w, h, d, other], dev(h, a + step, b))

    def d1_got(w, h, d, step, other):
        a, b = coords(h)
        y = 1 - yh if other else yh
        dst = piece(w, h, y, a - step, b)
        return remote(dst, dst, d1s.at[w, h, d, other], d1r.at[w, h, d, other], dev(h, a + step, b))

    def d2_copy(w, h, d, step):
        a, b = coords(h)
        ref = piece(w, h, d, a - step, b)
        return remote(ref, ref, d2s.at[w, h, d], d2r.at[w, h, d], dev(h, a + step, b))

    def d2_got(w, h, d, step):
        a, b = coords(h)
        ref = piece(w, h, d, a - 2 * step, b)
        return remote(ref, ref, d2s.at[w, h, d], d2r.at[w, h, d], dev(h, a + step, b))

    def e1_copy(w, h, d, step):
        a, b = coords(h)
        return remote(panels(w, h, b), panels(w, h, b), e1s.at[w, h, d], e1r.at[w, h, d], dev(h, a, b + step))

    def e1_got(w, h, d, step):
        a, b = coords(h)
        ref = panels(w, h, b - step)
        return remote(ref, ref, e1s.at[w, h, d], e1r.at[w, h, d], dev(h, a, b + step))

    def e2_copy(w, h, d, step):
        a, b = coords(h)
        ref = panel(w, h, d, b - step)
        return remote(ref, ref, e2s.at[w, h, d], e2r.at[w, h, d], dev(h, a, b + step))

    def e2_got(w, h, d, step):
        a, b = coords(h)
        ref = panel(w, h, d, b - 2 * step)
        return remote(ref, ref, e2s.at[w, h, d], e2r.at[w, h, d], dev(h, a, b + step))

    def own_shard(w, h):
        a, b = coords(h)
        return pltpu.make_async_copy(shard(w, h), piece(w, h, yh, a, b), os.at[w, h])

    def feat_copy():
        return remote(owned.at[pl.ds(tok - 8, 8)], feat, fs, fr, after)

    def halo_copy(t):
        return remote(
            gate.at[t, pl.ds(tok, BLOCK)], gate.at[t, pl.ds(0, BLOCK)], hs.at[t], hr.at[t], after
        )

    def part(c, k):
        return gated.at[c, :, pl.ds(pl.multiple_of(k * CHUNK, CHUNK), CHUNK)]

    def near_copy(k):
        return remote(part(ctx, k), part(ctx, k), ss.at[k], sr.at[k], sib)

    def near_got(k):
        return remote(part(ctx ^ 1, k), part(ctx ^ 1, k), ss.at[k], sr.at[k], sib)

    def far_copy(k):
        return remote(part(ctx, k), part(ctx, k), ns.at[k], nr.at[k], nb)

    def far_got(k):
        return remote(part(ctx ^ 2, k), part(ctx ^ 2, k), ns.at[k], nr.at[k], nb)

    def hand_copy(k):
        return remote(part(ctx ^ 2, k), part(ctx ^ 2, k), gs.at[k], gr.at[k], sib)

    def hand_got(k):
        return remote(part(ctx ^ 3, k), part(ctx ^ 3, k), gs.at[k], gr.at[k], sib)

    def out_at(c, w, h):
        start = pl.multiple_of(c * (WAVES * CHUNK) + w * CHUNK + h * TILE, TILE)
        return out.at[:, pl.ds(start, TILE)]

    def c_copy(w, h, c):
        return remote(staged.at[w, h, c], out_at(ctx, w, h), cs.at[w, h, c], cr.at[w, h, ctx], (fsdp, c))

    def c_got(w, h, c):
        return remote(staged.at[w, h, c], out_at(c, w, h), cs.at[w, h, c], cr.at[w, h, c], (fsdp, c))

    def c_own(w, h):
        return pltpu.make_async_copy(staged.at[w, h, ctx], out_at(ctx, w, h), cs.at[w, h, ctx])

    def band_copy(t, b):
        slot = (2 * t + b) % BUFFERS
        return pltpu.make_async_copy(bands.at[t, b], band_buf.at[slot], bs.at[slot])

    barrier = pltpu.get_barrier_semaphore()
    friends = [sib, nb, (fsdp, ctx ^ 3), partner]
    friends += [dev(0, xc + 1, zc), dev(0, xc - 1, zc), dev(0, xc, zc + 1), dev(0, xc, zc - 1)]
    for friend in friends:
        pl.semaphore_signal(barrier, inc=1, device_id=friend, device_id_type=MESH)
    pl.semaphore_wait(barrier, len(friends))

    feat_copy().start()
    rows_copy = pltpu.make_async_copy(owned, rows, ls)
    rows_copy.start()
    for i in range(BUFFERS):
        band_copy(i // 2, i % 2).start()
    for w, h in halves:
        y_copy(w, h).start()
        for d, step in ways:
            d1_copy(w, h, d, step, 0).start()
    for w, h in halves:
        own_shard(w, h).start()
    rows_copy.wait()
    feat_copy().wait_recv()

    lane_group = lax.broadcasted_iota(jnp.int32, (BLOCK, TILE), 1) // GROUP

    def expand(slot, column):
        xk[slot, pl.ds(0, 8), :] = feat[:, pl.ds(column, TILE)].astype(jnp.float32)
        xk[slot, pl.ds(8, tok), :] = rows[:, pl.ds(column, TILE)].astype(jnp.float32)

    def short(slot, column, b, lanes):
        total = None
        for i in range(TAPS):
            tap = short_full[i, pl.ds(pl.multiple_of(column + lanes, BLOCK), BLOCK)][None, :]
            term = xk[slot, pl.ds(8 + b * BLOCK - i, BLOCK), lanes : lanes + BLOCK] * tap
            if i > 0:
                term = term * short_mask[i - 1, b * BLOCK : (b + 1) * BLOCK, :]
            total = term if total is None else total + term
        return total

    def make_gate(t):
        key = pl.multiple_of(channels + t * TILE, TILE)
        value = pl.multiple_of(2 * channels + t * TILE, TILE)
        expand(0, key)
        expand(1, value)
        for b in range(2):
            for lanes in range(0, TILE, BLOCK):
                product = short(0, key, b, lanes) * short(1, value, b, lanes)
                gate[t, pl.ds((b + 1) * BLOCK, BLOCK), lanes : lanes + BLOCK] = product.astype(jnp.bfloat16)
        halo_copy(t).start()

    def convolve(t):
        query = pl.multiple_of(t * TILE, TILE)
        expand(2, query)
        halo_copy(t).wait_recv()
        for b in range(2):
            band_copy(t, b).wait()
            slot = (2 * t + b) % BUFFERS
            spread = jnp.dot(
                band_buf[slot], gate[t, pl.ds(b * BLOCK, 2 * BLOCK), :], preferred_element_type=jnp.float32
            )
            medium = spread[0:BLOCK]
            for j in range(1, GROUP):
                medium = jnp.where(lane_group == j, spread[j * BLOCK : (j + 1) * BLOCK], medium)
            for lanes in range(0, TILE, BLOCK):
                done = short(2, query, b, lanes) * medium[:, lanes : lanes + BLOCK]
                start = pl.multiple_of(query + lanes, BLOCK)
                gated[ctx, b * BLOCK : (b + 1) * BLOCK, pl.ds(start, BLOCK)] = done.astype(jnp.bfloat16)

            @pl.when(t + BUFFERS // 2 < tiles)
            def _():
                band_copy(t + BUFFERS // 2, b).start()

    lead = 2
    for t in range(lead):
        make_gate(t)

    for w, h in halves:
        y_got(w, h).wait_recv()
        for d, step in ways:
            d1_copy(w, h, d, step, 1).start()

    def weight_two():
        for w, h in halves:
            for d, step in ways:
                d1_got(w, h, d, step, 0).wait_recv()
                d1_got(w, h, d, step, 1).wait_recv()
                d2_copy(w, h, d, step).start()

    def weight_three(w):
        for h in range(2):
            own_shard(w, h).wait()
            for d, step in ways:
                d2_got(w, h, d, step).wait_recv()
        for h in range(2):
            for d, step in ways:
                e1_copy(w, h, d, step).start()

    def weight_four(w):
        for h in range(2):
            for d, step in ways:
                e1_got(w, h, d, step).wait_recv()
                e2_copy(w, h, d, step).start()

    def weight_done(w):
        for h in range(2):
            for d, step in ways:
                e2_got(w, h, d, step).wait_recv()

    def hand_on(k):
        far_got(k).wait_recv()
        hand_copy(k).start()

    def one_chunk(k, carry):
        def one_tile(i, carry):
            t = 2 * k + i

            @pl.when(t + lead < tiles)
            def _():
                make_gate(t + lead)

            convolve(t)
            return carry

        lax.fori_loop(0, 2, one_tile, 0)
        far_copy(k).start()
        near_copy(k).start()

        @pl.when(k == 1)
        def _():
            weight_two()

        @pl.when(k == 3)
        def _():
            weight_three(0)
            weight_three(1)

        @pl.when(k == 5)
        def _():
            weight_three(2)

        return carry

    lax.fori_loop(0, chunks, one_chunk, 0)

    for k in range(4):
        hand_on(k)
    weight_four(0)
    weight_three(3)
    hand_on(4)
    weight_four(1)
    hand_on(5)
    hand_on(6)
    weight_four(2)
    hand_on(7)
    for k in range(chunks):
        near_got(k).wait_recv()
        hand_got(k).wait_recv()

    mine = ctx // 2

    def multiply(w):
        def one_half(h, carry):
            cols = w_all[w, h].reshape(channels, TILE)
            for far in (1, 0):
                base = 2 * ((mine + far) % 2)
                lhs = gated[pl.ds(base, 2)].reshape(2 * tok, channels)
                product = jnp.dot(lhs, cols, preferred_element_type=jnp.float32)
                staged[w, h, pl.ds(base, 2)] = product.astype(jnp.bfloat16).reshape(2, tok, TILE)
                if far:
                    c_copy(w, h, base).start()
                    c_copy(w, h, base + 1).start()
                else:
                    c_copy(w, h, ctx ^ 1).start()
                    c_own(w, h).start()
            return carry

        lax.fori_loop(0, 2, one_half, 0)

    for w in range(WAVES):
        weight_done(w)
        multiply(w)
        if w == 0:
            weight_four(3)

    feat_copy().wait_send()
    for w, h in halves:
        y_copy(w, h).wait_send()
        for d, step in ways:
            for other in range(2):
                d1_copy(w, h, d, step, other).wait_send()
            d2_copy(w, h, d, step).wait_send()
            e1_copy(w, h, d, step).wait_send()
            e2_copy(w, h, d, step).wait_send()
    for t in range(tiles):
        halo_copy(t).wait_send()
    for k in range(chunks):
        far_copy(k).wait_send()
        near_copy(k).wait_send()
        hand_copy(k).wait_send()
    for w, h in halves:
        c_own(w, h).wait()
        for flip in (1, 2, 3):
            c_copy(w, h, ctx ^ flip).wait_send()
            c_got(w, h, ctx ^ flip).wait_recv()


def mix(owned, bands, short_mask, short_full, weight):
    tok, wide = owned.shape
    channels = wide // 3
    depth, columns = weight.shape
    tiles, chunks = channels // TILE, channels // CHUNK
    dma = pltpu.SemaphoreType.DMA
    vmem, anywhere = pl.BlockSpec(memory_space=pltpu.VMEM), pl.BlockSpec(memory_space=pl.ANY)
    return pl.pallas_call(
        mixer_kernel,
        out_shape=jax.ShapeDtypeStruct((tok, 4 * columns), jnp.bfloat16),
        in_specs=[anywhere, anywhere, vmem, vmem, anywhere],
        out_specs=anywhere,
        scratch_shapes=[
            pltpu.VMEM((WAVES, 2, 2, RING, RING, depth, TILE), jnp.bfloat16),
            pltpu.VMEM((4, tok, channels), jnp.bfloat16),
            pltpu.VMEM((WAVES, 2, 4, tok, TILE), jnp.bfloat16),
            pltpu.VMEM((tok, wide), jnp.bfloat16),
            pltpu.VMEM((8, wide), jnp.bfloat16),
            pltpu.VMEM((tiles, tok + BLOCK, TILE), jnp.bfloat16),
            pltpu.VMEM((3, tok + 8, TILE), jnp.float32),
            pltpu.VMEM((BUFFERS, GROUP * BLOCK, 2 * BLOCK), jnp.bfloat16),
            dma((WAVES, 2)), dma((WAVES, 2)),
            dma((WAVES, 2, 2, 2)), dma((WAVES, 2, 2, 2)),
            dma((WAVES, 2, 2)), dma((WAVES, 2, 2)),
            dma((WAVES, 2, 2)), dma((WAVES, 2, 2)),
            dma((WAVES, 2, 2)), dma((WAVES, 2, 2)),
            dma(()), dma(()),
            dma((tiles,)), dma((tiles,)),
            dma((chunks,)), dma((chunks,)),
            dma((chunks,)), dma((chunks,)),
            dma((chunks,)), dma((chunks,)),
            dma((WAVES, 2, 4)), dma((WAVES, 2, 4)),
            dma(()), dma((BUFFERS,)), dma((WAVES, 2)),
        ],
        compiler_params=pltpu.CompilerParams(
            vmem_limit_bytes=VMEM_LIMIT, collective_id=0, has_side_effects=True
        ),
        name="mixer",
    )(owned, bands, short_mask, short_full, weight)


def on_device(loaded, route, doc_ids, short_filter, medium_filter, out_weight):
    tok, wide = loaded.shape
    fsdp_count = lax.axis_size("fsdp")
    blk = tok // fsdp_count
    group = wide // short_filter.shape[1]
    taps = medium_filter.shape[0]

    slots = jnp.arange(fsdp_count, dtype=jnp.int32)
    order = jnp.sum(jnp.where(route[0][None, :] == slots[:, None], slots[None, :], 0), axis=1).astype(jnp.int32)
    picked = pick_blocks(order, loaded.reshape(fsdp_count, blk, wide))
    owned = lax.all_to_all(picked, "fsdp", split_axis=0, concat_axis=0, tiled=True).reshape(tok, wide)

    ids = jnp.concatenate([jnp.full((BLOCK,), -1, jnp.int32), doc_ids[0]], axis=0)
    near_ids = lax.dynamic_slice_in_dim(ids, lax.axis_index("ctx") * tok, tok + BLOCK, 0)
    own_ids = near_ids[BLOCK:]
    short_mask = jnp.stack(
        [
            jnp.broadcast_to((near_ids[BLOCK - i : BLOCK - i + tok] == own_ids)[:, None], (tok, BLOCK))
            for i in range(1, TAPS)
        ]
    ).astype(jnp.float32)
    short_full = jnp.pad(jnp.repeat(short_filter, group, axis=1), ((0, 1), (0, 0)))
    mask = jnp.stack(
        [
            own_ids[b * BLOCK : (b + 1) * BLOCK, None] == near_ids[None, b * BLOCK : (b + 2) * BLOCK]
            for b in range(2)
        ]
    ).astype(jnp.float32)
    base = jnp.pad(medium_filter[::-1].T.astype(jnp.float32), ((0, 0), (1, 2 * BLOCK - 1 - taps)))
    bands = build_bands(base, mask)
    return mix(owned, bands, short_mask, short_full, out_weight)


def solution(mesh):
    placed = (
        P(("fsdp", "ctx"), None),
        P(("fsdp", "ctx"), None),
        P("fsdp", None),
        P(),
        P(),
        P("fsdp", "ctx"),
    )
    return jax.shard_map(
        on_device, mesh=mesh, in_specs=placed, out_specs=P(("fsdp", "ctx"), None), check_vma=False
    )
```

```python
import functools

import jax
import jax.numpy as jnp
from jax import lax
from jax.experimental import pallas as pl
from jax.experimental.pallas import tpu as pltpu
from jax.sharding import PartitionSpec as P

MESH = pl.DeviceIdType.MESH
VMEM_LIMIT = 66_000_000
RING = 4
WAVES = 4
TILE = 256
BLOCK = 128
GROUP = 16
TAPS = 7
CHUNK = 512
BUFFERS = 4


def pick_kernel(route, loaded, picked, held, load_sem, store_sem):
    blocks = loaded.shape[0]
    chunks = picked.shape[0]

    def load(i):
        return pltpu.make_async_copy(loaded.at[i], held.at[i], load_sem.at[i])

    def store(i, k, j):
        column = j * chunks * CHUNK + k * CHUNK
        return pltpu.make_async_copy(
            held.at[i, :, pl.ds(column, CHUNK)],
            picked.at[k, route[0, i], :, pl.ds(j * CHUNK, CHUNK)],
            store_sem.at[i, k, j],
        )

    @pl.loop(0, blocks)
    def _(i):
        load(i).start()

    @pl.loop(0, blocks)
    def _(i):
        load(i).wait()
        for k in range(chunks):
            for j in range(3):
                store(i, k, j).start()

    @pl.loop(0, blocks)
    def _(i):
        for k in range(chunks):
            for j in range(3):
                store(i, k, j).wait()


def pick_blocks(route, loaded):
    blocks, rows, wide = loaded.shape
    chunks = wide // (3 * CHUNK)
    return pl.pallas_call(
        pick_kernel,
        out_shape=jax.ShapeDtypeStruct((chunks, blocks, rows, 3 * CHUNK), loaded.dtype),
        in_specs=[
            pl.BlockSpec(memory_space=pltpu.SMEM),
            pl.BlockSpec(memory_space=pl.ANY),
        ],
        out_specs=pl.BlockSpec(memory_space=pl.ANY),
        scratch_shapes=[
            pltpu.VMEM((blocks, rows, wide), loaded.dtype),
            pltpu.SemaphoreType.DMA((blocks,)),
            pltpu.SemaphoreType.DMA((blocks, chunks, 3)),
        ],
        compiler_params=pltpu.CompilerParams(vmem_limit_bytes=VMEM_LIMIT),
        name="pick_blocks",
    )(route, loaded)


def mixer_kernel(
    picked, doc_ids, short_filter, medium_filter, weight, out,
    w_all, gated, staged, rows, feat, gate, xk, bands,
    taps, short_full, base, id_rows, id_columns, short_mask, band_mask,
    xs, xr, xo,
    ys, yr, d1s, d1r, d2s, d2r, e1s, e1r, e2s, e2r,
    fs, fr, hs, hr, ns, nr, ss, sr, gs, gr, cs, cr, os,
):
    fsdp, ctx = lax.axis_index("fsdp"), lax.axis_index("ctx")
    yh, zc, xc = fsdp // (RING * RING), (fsdp // RING) % RING, fsdp % RING
    sib, nb = (fsdp, ctx ^ 1), (fsdp, ctx ^ 2)
    after, before = (fsdp, (ctx + 1) % 4), (fsdp, (ctx + 3) % 4)
    partner = ((1 - yh) * RING * RING + zc * RING + xc, ctx)
    channels = gated.shape[2]
    tiles = channels // TILE
    chunks = channels // CHUNK
    blocks, blk = rows.shape[1], rows.shape[2]
    tok = blocks * blk

    def coords(h):
        return (xc, zc) if h == 0 else (zc, xc)

    def dev(h, a, b):
        a, b = (a + RING) % RING, (b + RING) % RING
        z, x = (b, a) if h == 0 else (a, b)
        return (yh * RING * RING + z * RING + x, ctx)

    def piece(w, h, y, a, b):
        a, b = (a + RING) % RING, (b + RING) % RING
        z, x = (b, a) if h == 0 else (a, b)
        return w_all.at[w, h, y, z, x]

    def panel(w, h, y, b):
        b = (b + RING) % RING
        if h == 0:
            return w_all.at[w, h, y, b]
        return w_all.at[w, h, y, :, b]

    def panels(w, h, b):
        b = (b + RING) % RING
        if h == 0:
            return w_all.at[w, h, :, b]
        return w_all.at[w, h, :, :, b]

    def shard(w, h):
        return weight.at[:, pl.ds(w * CHUNK + h * TILE, TILE)]

    def remote(src, dst, send, recv, to):
        return pltpu.make_async_remote_copy(
            src_ref=src, dst_ref=dst, send_sem=send, recv_sem=recv, device_id=to, device_id_type=MESH
        )

    halves = [(w, h) for w in range(WAVES) for h in range(2)]
    ways = ((0, 1), (1, -1))

    def y_copy(w, h):
        a, b = coords(h)
        return remote(shard(w, h), piece(w, h, yh, a, b), ys.at[w, h], yr.at[w, h], partner)

    def y_got(w, h):
        a, b = coords(h)
        return remote(shard(w, h), piece(w, h, 1 - yh, a, b), ys.at[w, h], yr.at[w, h], partner)

    def d1_copy(w, h, d, step, other):
        a, b = coords(h)
        y = 1 - yh if other else yh
        src = piece(w, h, y, a, b) if other else shard(w, h)
        return remote(src, piece(w, h, y, a, b), d1s.at[w, h, d, other], d1r.at[w, h, d, other], dev(h, a + step, b))

    def d1_got(w, h, d, step, other):
        a, b = coords(h)
        y = 1 - yh if other else yh
        dst = piece(w, h, y, a - step, b)
        return remote(dst, dst, d1s.at[w, h, d, other], d1r.at[w, h, d, other], dev(h, a + step, b))

    def d2_copy(w, h, d, step):
        a, b = coords(h)
        ref = piece(w, h, d, a - step, b)
        return remote(ref, ref, d2s.at[w, h, d], d2r.at[w, h, d], dev(h, a + step, b))

    def d2_got(w, h, d, step):
        a, b = coords(h)
        ref = piece(w, h, d, a - 2 * step, b)
        return remote(ref, ref, d2s.at[w, h, d], d2r.at[w, h, d], dev(h, a + step, b))

    def e1_copy(w, h, d, step):
        a, b = coords(h)
        return remote(panels(w, h, b), panels(w, h, b), e1s.at[w, h, d], e1r.at[w, h, d], dev(h, a, b + step))

    def e1_got(w, h, d, step):
        a, b = coords(h)
        ref = panels(w, h, b - step)
        return remote(ref, ref, e1s.at[w, h, d], e1r.at[w, h, d], dev(h, a, b + step))

    def e2_copy(w, h, d, step):
        a, b = coords(h)
        ref = panel(w, h, d, b - step)
        return remote(ref, ref, e2s.at[w, h, d], e2r.at[w, h, d], dev(h, a, b + step))

    def e2_got(w, h, d, step):
        a, b = coords(h)
        ref = panel(w, h, d, b - 2 * step)
        return remote(ref, ref, e2s.at[w, h, d], e2r.at[w, h, d], dev(h, a, b + step))

    def own_shard(w, h):
        a, b = coords(h)
        return pltpu.make_async_copy(shard(w, h), piece(w, h, yh, a, b), os.at[w, h])

    def feat_copy(k):
        return remote(rows.at[k, blocks - 1], feat.at[k], fs.at[k], fr.at[k], after)

    def halo_copy(t):
        return remote(
            gate.at[t, pl.ds(tok, BLOCK)], gate.at[t, pl.ds(0, BLOCK)], hs.at[t], hr.at[t], after
        )

    def part(c, k):
        return gated.at[c, :, pl.ds(pl.multiple_of(k * CHUNK, CHUNK), CHUNK)]

    def near_copy(k):
        return remote(part(ctx, k), part(ctx, k), ss.at[k], sr.at[k], sib)

    def near_got(k):
        return remote(part(ctx ^ 1, k), part(ctx ^ 1, k), ss.at[k], sr.at[k], sib)

    def far_copy(k):
        return remote(part(ctx, k), part(ctx, k), ns.at[k], nr.at[k], nb)

    def far_got(k):
        return remote(part(ctx ^ 2, k), part(ctx ^ 2, k), ns.at[k], nr.at[k], nb)

    def hand_copy(k):
        return remote(part(ctx ^ 2, k), part(ctx ^ 2, k), gs.at[k], gr.at[k], sib)

    def hand_got(k):
        return remote(part(ctx ^ 3, k), part(ctx ^ 3, k), gs.at[k], gr.at[k], sib)

    def out_at(c, w, h):
        start = pl.multiple_of(c * (WAVES * CHUNK) + w * CHUNK + h * TILE, TILE)
        return out.at[:, pl.ds(start, TILE)]

    def c_copy(w, h, c):
        return remote(staged.at[w, h, c], out_at(ctx, w, h), cs.at[w, h, c], cr.at[w, h, ctx], (fsdp, c))

    def c_got(w, h, c):
        return remote(staged.at[w, h, c], out_at(c, w, h), cs.at[w, h, c], cr.at[w, h, c], (fsdp, c))

    def c_own(w, h):
        return pltpu.make_async_copy(staged.at[w, h, ctx], out_at(ctx, w, h), cs.at[w, h, ctx])

    others = [(y, z, x) for y in range(2) for z in range(RING) for x in range(RING)][1:]
    others.sort(key=lambda d: (d[0] * 7 + d[1] * 5 + d[2] * 3) % 11)

    def shifted(d):
        z, x = (zc + d[1]) % RING, (xc + d[2]) % RING
        return ((yh + d[0]) % 2) * RING * RING + z * RING + x

    def block_copy(k, d):
        to = shifted(d)
        return remote(picked.at[k, to], rows.at[k, fsdp], xs.at[k], xr.at[k], (to, ctx))

    def block_all(k):
        few = pl.ds(0, len(others))
        return remote(picked.at[k, few], rows.at[k, few], xs.at[k], xr.at[k], partner)

    def block_own(k):
        return pltpu.make_async_copy(picked.at[k, fsdp], rows.at[k, fsdp], xo.at[k])

    barrier = pltpu.get_barrier_semaphore()
    friends = [(shifted(d), ctx) for d in others] + [sib, nb, (fsdp, ctx ^ 3)]
    for friend in friends:
        pl.semaphore_signal(barrier, inc=1, device_id=friend, device_id_type=MESH)
    pl.semaphore_wait(barrier, len(friends))

    @pl.loop(0, chunks)
    def _(k):
        for d in others:
            block_copy(k, d).start()
        block_own(k).start()

    for w, h in halves:
        own_shard(w, h).start()

    start = jnp.maximum(ctx * tok - BLOCK, 0)
    first = doc_ids[:, pl.ds(pl.multiple_of(start, BLOCK), BLOCK)].astype(jnp.float32)
    id_rows[:, 0:BLOCK] = jnp.where(ctx > 0, first, -1.0)
    id_rows[:, BLOCK:] = doc_ids[:, pl.ds(pl.multiple_of(ctx * tok, tok), tok)].astype(jnp.float32)
    for m in range(3):
        spread_ids = jnp.broadcast_to(id_rows[:, m * BLOCK : (m + 1) * BLOCK], (BLOCK, BLOCK))
        id_columns[m * BLOCK : (m + 1) * BLOCK, :] = spread_ids.T
    for i in range(1, TAPS):
        same = id_columns[BLOCK - i : BLOCK - i + tok, :] == id_columns[BLOCK:, :]
        short_mask[i - 1] = same.astype(jnp.float32)
    for b in range(2):
        own_id = id_columns[(b + 1) * BLOCK : (b + 2) * BLOCK, :]
        for m in range(2):
            same = own_id == id_rows[:, (b + m) * BLOCK : (b + m + 1) * BLOCK]
            band_mask[b, :, m * BLOCK : (m + 1) * BLOCK] = same.astype(jnp.float32)
    depth = medium_filter.shape[0]
    tap_row = lax.broadcasted_iota(jnp.int32, (depth, 2 * BLOCK), 0)
    tap_column = lax.broadcasted_iota(jnp.int32, (depth, 2 * BLOCK), 1)
    flip = (tap_row + tap_column == depth).astype(jnp.bfloat16)
    base[...] = lax.dot_general(
        medium_filter[...], flip, (((0,), (0,)), ((), ())), preferred_element_type=jnp.float32
    )
    taps[...] = jnp.zeros_like(taps)
    taps[0:TAPS, :] = short_filter[...]
    group_row = lax.broadcasted_iota(jnp.int32, (BLOCK, CHUNK), 0)
    group_column = lax.broadcasted_iota(jnp.int32, (BLOCK, CHUNK), 1) // GROUP

    @pl.loop(0, 3 * chunks)
    def _(j):
        per = CHUNK // GROUP
        source = pl.multiple_of((j * per // BLOCK) * BLOCK, BLOCK)
        repeat = (group_row == group_column + j * per - source).astype(jnp.float32)
        short_full[:, pl.ds(pl.multiple_of(j * CHUNK, CHUNK), CHUNK)] = jnp.dot(
            taps[:, pl.ds(source, BLOCK)], repeat,
            precision=lax.Precision.HIGHEST, preferred_element_type=jnp.float32,
        )

    def build_bands(t):
        def one(j, carry):
            row = jnp.broadcast_to(base[pl.ds(t * GROUP + j, 1), :], (BLOCK, 2 * BLOCK))
            band = pltpu.roll(row, 0, 1, stride=1, stride_axis=0)
            first_row = pl.multiple_of(j * BLOCK, BLOCK)
            for b in range(2):
                bands[t % BUFFERS, b, pl.ds(first_row, BLOCK), :] = (band * band_mask[b]).astype(jnp.bfloat16)
            return carry

        lax.fori_loop(0, GROUP, one, 0)

    @pl.loop(0, BUFFERS)
    def _(t):
        build_bands(t)

    lane_group = lax.broadcasted_iota(jnp.int32, (BLOCK, TILE), 1) // GROUP

    def expand(slot, k, half, j):
        for l in range(TILE // BLOCK):
            column = pl.multiple_of(j * CHUNK + half * TILE + l * BLOCK, BLOCK)
            xk[slot, l, pl.ds(0, 8), :] = feat[k, :, pl.ds(column, BLOCK)].astype(jnp.float32)
            own = rows[k, :, :, pl.ds(column, BLOCK)].astype(jnp.float32)
            xk[slot, l, pl.ds(8, tok), :] = own.reshape(tok, BLOCK)

    def short(slot, column, b, l):
        total = None
        for i in range(TAPS):
            tap = short_full[i, pl.ds(pl.multiple_of(column + l * BLOCK, BLOCK), BLOCK)][None, :]
            term = xk[slot, l, pl.ds(8 + b * BLOCK - i, BLOCK), :] * tap
            if i > 0:
                term = term * short_mask[i - 1, b * BLOCK : (b + 1) * BLOCK, :]
            total = term if total is None else total + term
        return total

    def make_gate(k, half):
        t = 2 * k + half
        key = pl.multiple_of(channels + t * TILE, TILE)
        value = pl.multiple_of(2 * channels + t * TILE, TILE)
        expand(0, k, half, 1)
        expand(1, k, half, 2)
        for b in range(2):
            for l in range(TILE // BLOCK):
                product = short(0, key, b, l) * short(1, value, b, l)
                gate[t, pl.ds((b + 1) * BLOCK, BLOCK), l * BLOCK : (l + 1) * BLOCK] = product.astype(jnp.bfloat16)
        halo_copy(t).start()

    def convolve(k, half):
        t = 2 * k + half
        query = pl.multiple_of(t * TILE, TILE)
        expand(2, k, half, 0)
        halo_copy(t).wait_recv()
        for b in range(2):
            spread = jnp.dot(
                bands[t % BUFFERS, b], gate[t, pl.ds(b * BLOCK, 2 * BLOCK), :], preferred_element_type=jnp.float32
            )
            medium = spread[0:BLOCK]
            for j in range(1, GROUP):
                medium = jnp.where(lane_group == j, spread[j * BLOCK : (j + 1) * BLOCK], medium)
            for l in range(TILE // BLOCK):
                done = short(2, query, b, l) * medium[:, l * BLOCK : (l + 1) * BLOCK]
                at = pl.multiple_of(query + l * BLOCK, BLOCK)
                gated[ctx, b * BLOCK : (b + 1) * BLOCK, pl.ds(at, BLOCK)] = done.astype(jnp.bfloat16)

        @pl.when(t + BUFFERS < tiles)
        def _():
            build_bands(t + BUFFERS)

    def weight_one():
        for w, h in halves:
            y_copy(w, h).start()
            for d, step in ways:
                d1_copy(w, h, d, step, 0).start()

    def weight_other():
        for w, h in halves:
            y_got(w, h).wait_recv()
            for d, step in ways:
                d1_copy(w, h, d, step, 1).start()

    def weight_two():
        for w, h in halves:
            for d, step in ways:
                d1_got(w, h, d, step, 0).wait_recv()
                d1_got(w, h, d, step, 1).wait_recv()
                d2_copy(w, h, d, step).start()

    def weight_three(w):
        for h in range(2):
            own_shard(w, h).wait()
            for d, step in ways:
                d2_got(w, h, d, step).wait_recv()
        for h in range(2):
            for d, step in ways:
                e1_copy(w, h, d, step).start()

    def weight_four(w):
        for h in range(2):
            for d, step in ways:
                e1_got(w, h, d, step).wait_recv()
                e2_copy(w, h, d, step).start()

    def weight_done(w):
        for h in range(2):
            for d, step in ways:
                e2_got(w, h, d, step).wait_recv()

    def hand_on(k):
        far_got(k).wait_recv()
        hand_copy(k).start()

    @pl.loop(0, chunks + 2)
    def _(k):
        @pl.when(k < chunks)
        def _():
            block_all(k).wait_recv()
            block_own(k).wait()
            feat_copy(k).start()

        @pl.when(k == 4)
        def _():
            weight_one()

        @pl.when(k == 5)
        def _():
            weight_other()

        @pl.when(k == 6)
        def _():
            weight_two()

        @pl.when(k == 7)
        def _():
            weight_three(0)
            weight_three(1)

        @pl.when(k == 8)
        def _():
            weight_three(2)

        @pl.when((k > 0) & (k <= chunks))
        def _():
            feat_copy(k - 1).wait_recv()

            @pl.loop(0, 2)
            def _(half):
                make_gate(k - 1, half)

        @pl.when(k > 1)
        def _():
            @pl.loop(0, 2)
            def _(half):
                convolve(k - 2, half)

            far_copy(k - 2).start()
            near_copy(k - 2).start()

    for k in range(4):
        hand_on(k)
    weight_four(0)
    weight_three(3)
    hand_on(4)
    weight_four(1)
    hand_on(5)
    hand_on(6)
    weight_four(2)
    hand_on(7)
    for k in range(chunks):
        near_got(k).wait_recv()
        hand_got(k).wait_recv()

    mine = ctx // 2

    def multiply(w):
        def one_half(h, carry):
            cols = w_all[w, h].reshape(channels, TILE)
            for far in (1, 0):
                base = 2 * ((mine + far) % 2)
                lhs = gated[pl.ds(base, 2)].reshape(2 * tok, channels)
                product = jnp.dot(lhs, cols, preferred_element_type=jnp.float32)
                staged[w, h, pl.ds(base, 2)] = product.astype(jnp.bfloat16).reshape(2, tok, TILE)
                if far:
                    c_copy(w, h, base).start()
                    c_copy(w, h, base + 1).start()
                else:
                    c_copy(w, h, ctx ^ 1).start()
                    c_own(w, h).start()
            return carry

        lax.fori_loop(0, 2, one_half, 0)

    for w in range(WAVES):
        weight_done(w)
        multiply(w)
        if w == 1:
            weight_four(3)

    for k in range(chunks):
        block_all(k).wait_send()
        feat_copy(k).wait_send()
    for w, h in halves:
        y_copy(w, h).wait_send()
        for d, step in ways:
            for other in range(2):
                d1_copy(w, h, d, step, other).wait_send()
            d2_copy(w, h, d, step).wait_send()
            e1_copy(w, h, d, step).wait_send()
            e2_copy(w, h, d, step).wait_send()
    for t in range(tiles):
        halo_copy(t).wait_send()
    for k in range(chunks):
        far_copy(k).wait_send()
        near_copy(k).wait_send()
        hand_copy(k).wait_send()
    for w, h in halves:
        c_own(w, h).wait()
        for flip in (1, 2, 3):
            c_copy(w, h, ctx ^ flip).wait_send()
            c_got(w, h, ctx ^ flip).wait_recv()


def mix(picked, doc_ids, short_filter, medium_filter, weight):
    chunks, blocks, blk, triple = picked.shape
    tok, channels = blocks * blk, chunks * triple // 3
    depth, columns = weight.shape
    tiles, groups = channels // TILE, medium_filter.shape[1]
    dma = pltpu.SemaphoreType.DMA
    vmem, anywhere = pl.BlockSpec(memory_space=pltpu.VMEM), pl.BlockSpec(memory_space=pl.ANY)
    return pl.pallas_call(
        mixer_kernel,
        out_shape=jax.ShapeDtypeStruct((tok, 4 * columns), jnp.bfloat16),
        in_specs=[anywhere, vmem, vmem, vmem, anywhere],
        out_specs=anywhere,
        scratch_shapes=[
            pltpu.VMEM((WAVES, 2, 2, RING, RING, depth, TILE), jnp.bfloat16),
            pltpu.VMEM((4, tok, channels), jnp.bfloat16),
            pltpu.VMEM((WAVES, 2, 4, tok, TILE), jnp.bfloat16),
            pltpu.VMEM(picked.shape, jnp.bfloat16),
            pltpu.VMEM((chunks, blk, triple), jnp.bfloat16),
            pltpu.VMEM((tiles, tok + BLOCK, TILE), jnp.bfloat16),
            pltpu.VMEM((3, TILE // BLOCK, tok + 8, BLOCK), jnp.float32),
            pltpu.VMEM((BUFFERS, 2, GROUP * BLOCK, 2 * BLOCK), jnp.bfloat16),
            pltpu.VMEM((8, short_filter.shape[1]), jnp.float32),
            pltpu.VMEM((8, 3 * channels), jnp.float32),
            pltpu.VMEM((groups, 2 * BLOCK), jnp.float32),
            pltpu.VMEM((1, 3 * BLOCK), jnp.float32),
            pltpu.VMEM((3 * BLOCK, BLOCK), jnp.float32),
            pltpu.VMEM((TAPS - 1, tok, BLOCK), jnp.float32),
            pltpu.VMEM((2, BLOCK, 2 * BLOCK), jnp.float32),
            dma((chunks,)), dma((chunks,)), dma((chunks,)),
            dma((WAVES, 2)), dma((WAVES, 2)),
            dma((WAVES, 2, 2, 2)), dma((WAVES, 2, 2, 2)),
            dma((WAVES, 2, 2)), dma((WAVES, 2, 2)),
            dma((WAVES, 2, 2)), dma((WAVES, 2, 2)),
            dma((WAVES, 2, 2)), dma((WAVES, 2, 2)),
            dma((chunks,)), dma((chunks,)),
            dma((tiles,)), dma((tiles,)),
            dma((chunks,)), dma((chunks,)),
            dma((chunks,)), dma((chunks,)),
            dma((chunks,)), dma((chunks,)),
            dma((WAVES, 2, 4)), dma((WAVES, 2, 4)),
            dma((WAVES, 2)),
        ],
        compiler_params=pltpu.CompilerParams(
            vmem_limit_bytes=VMEM_LIMIT, collective_id=0, has_side_effects=True
        ),
        name="mixer",
    )(picked, doc_ids, short_filter, medium_filter, weight)


def on_device(loaded, route, doc_ids, short_filter, medium_filter, out_weight):
    tok, wide = loaded.shape
    blocks = route.shape[1]
    picked = pick_blocks(route, loaded.reshape(blocks, tok // blocks, wide))
    return mix(picked, doc_ids, short_filter, medium_filter, out_weight)


def solution(mesh):
    placed = (
        P(("fsdp", "ctx"), None),
        P(("fsdp", "ctx"), None),
        P("fsdp", None),
        P(),
        P(),
        P("fsdp", "ctx"),
    )
    return jax.shard_map(
        on_device, mesh=mesh, in_specs=placed, out_specs=P(("fsdp", "ctx"), None), check_vma=False
    )
```
